32 devices in a mesh: dp: 2 (over x), expert: 16 (over z, y, core).
Axes of the slice: x: 2, y: 2, z: 4, core: 2. Of those that a mesh axis runs over, the one named last changes fastest.
Arguments:
- tokens: bfloat16 [4096, 7168], P('expert', 'dp'), may hold values from -6 to 6
- cotangent: bfloat16 [4096, 7168], P('expert', 'dp'), may hold values from -6 to 6
- routing: int32 [4096, 8], P('expert'), may hold values from 0 to 255, as said below
- gate_values: float32 [4096, 8], P('expert'), may hold values from 0.05 to 0.6
- hidden_weight: bfloat16 [16, 7168, 2048], P('expert', 'dp'), may hold values from -0.0625 to 0.0625
- output_weight: bfloat16 [16, 1024, 7168], P('expert', None, 'dp'), may hold values from -0.1875 to 0.1875
Outputs:
- mixed: bfloat16 [4096, 7168], P('expert', 'dp')
- token_grad: bfloat16 [4096, 7168], P('expert', 'dp')
- hidden_grad: bfloat16 [16, 7168, 2048], P('expert', 'dp')
- output_grad: bfloat16 [16, 1024, 7168], P('expert', None, 'dp')
The draws below stay inside these ranges and needn't reach their ends.
Inputs may be any that keep to these rules, and one draw needn't show every extreme that they name: `routing`: each row names 8 different experts. Within the 256 rows of one index of expert no expert is named by more than 16 rows, and in every such block some experts below 16 are named by exactly 16 rows.
All inputs are finite; a program needn't handle non-finite values.
Results may differ from the reference program's by a relative error of at most 0.022.
Values may be sent and summed in bfloat16 or wider, within the bound.
No kernel may reach another device: no remote copies, remote signals or barrier semaphores. Data moves between devices by JAX's collectives and lax.ppermute only.
A program may use at most 128 MiB of HBM per device.

```python
import jax
import jax.numpy as jnp
from jax import lax

D = 7168
FFW = 1024
TOP = 8
ROUTED = 256
TOK_DEV = 256
EXPERTS = 16
SLOTS = 16
TOKENS = 4096
N_DP = 2


def draw_routing(key, part):
    blocks = TOKENS // TOK_DEV
    half_count = ROUTED // 2
    ranked_ids = jax.random.permutation(jax.random.fold_in(key, 11), EXPERTS)
    hot_mask = jnp.any(jnp.arange(EXPERTS, dtype=jnp.int32)[:, None] == ranked_ids[None, :3], axis=1)
    levels = jax.random.randint(jax.random.fold_in(key, 12), (blocks, half_count), 0, SLOTS)
    window_level = jax.random.randint(jax.random.fold_in(key, 13), (blocks, EXPERTS), 0, SLOTS)
    window_level = jnp.where(hot_mask[None, :], SLOTS, window_level)
    first_count = jnp.concatenate([window_level, levels[:, EXPERTS:]], axis=1)
    counts = jnp.concatenate([first_count, SLOTS - first_count], axis=1)
    expert_ids = jnp.arange(ROUTED, dtype=jnp.int32)

    def fill_block(count_row, block_key):
        pick_list = jnp.repeat(expert_ids, count_row, total_repeat_length=TOK_DEV * TOP)
        pick_table = pick_list.reshape(TOP, TOK_DEV).T
        shuffled = jax.random.permutation(block_key, TOK_DEV)
        return pick_table[shuffled]
    block_keys = jax.random.split(jax.random.fold_in(key, 14), blocks)
    return jax.vmap(fill_block)(counts, block_keys).reshape(TOKENS, TOP).astype(jnp.int32)


def level_of(key, shape, cuts, low, high):
    gain, own = 1.0, jax.random.fold_in(key, 6)
    for axis_at, parts in cuts:
        steps = jnp.exp(jax.random.uniform(jax.random.fold_in(own, axis_at), (parts,), jnp.float32, low / len(cuts), high / len(cuts)))
        gain = gain * jnp.repeat(steps, shape[axis_at] // parts).reshape([-1 if axis == axis_at else 1 for axis in range(len(shape))])
    return gain


def bell_draw(own_key, dims, deviation, reach, cuts=(), kind=jnp.bfloat16):
    gain = level_of(own_key, dims, cuts, -0.22, 0.18) if cuts else 1.0
    drawn = jax.random.normal(own_key, dims, jnp.float32) * deviation * gain
    return jnp.minimum(jnp.maximum(drawn, -reach), reach).astype(kind)


def setup_inputs(seed: int = 0) -> dict:
    keys = jax.random.split(jax.random.key(seed), 7)
    tokens = bell_draw(keys[0], (TOKENS, D), 1.0, 6.0, ((0, 16), (1, 2)))
    cotangent = bell_draw(keys[1], (TOKENS, D), 1.0, 6.0, ((0, 16), (1, 2)))
    routing = draw_routing(jax.random.fold_in(keys[6], 71), 0)
    gate_values = jnp.clip(0.05 + 0.55 * jax.random.uniform(keys[3], (TOKENS, TOP), jnp.float32) ** level_of(keys[3], (TOKENS, TOP), ((0, 16),), -0.2, 0.2), 0.05, 0.6)
    hidden_weight = bell_draw(keys[4], (EXPERTS, D, 2 * FFW), D ** -0.5, 0.0625, ((0, 16), (1, 2)))
    output_weight = bell_draw(keys[5], (EXPERTS, FFW, D), FFW ** -0.5, 0.1875, ((0, 16), (2, 2)))
    return {"tokens": tokens, "cotangent": cotangent, "routing": routing, "gate_values": gate_values, "hidden_weight": hidden_weight, "output_weight": output_weight}


def slot_table(routing_block, gate_block, expert_count, slot_count):
    tok_count = routing_block.shape[0]
    picked = routing_block.reshape(-1)
    onehot = (picked[:, None] == jnp.arange(expert_count, dtype=jnp.int32)[None, :]).astype(jnp.int32)
    earlier = jnp.cumsum(onehot, axis=0) - onehot
    ranking = lax.optimization_barrier(jnp.sum(earlier * onehot, axis=1))
    slot_index = (picked * slot_count + ranking).reshape(tok_count, -1)
    target = jnp.arange(expert_count * slot_count, dtype=jnp.int32)
    matched = slot_index[None, :, :] == target[:, None, None]
    placed = jnp.any(matched, axis=2).astype(jnp.float32)
    gate_slot = lax.optimization_barrier(jnp.sum(jnp.where(matched, gate_block[None, :, :], jnp.zeros_like(gate_block)[None, :, :]), axis=(1, 2)))
    return (placed, gate_slot)

def activate(hidden, half_width):
    gate_part = hidden[:, :half_width]
    up_part = hidden[:, half_width:]
    return (gate_part * jax.nn.sigmoid(gate_part) * up_part).astype(jnp.bfloat16)

def activate_grad(hidden, act_grad, half_width):
    gate_part = hidden[:, :half_width]
    up_part = hidden[:, half_width:]
    sigmoid_gate = jax.nn.sigmoid(gate_part)
    gate_grad = act_grad * up_part * sigmoid_gate * (1.0 + gate_part * (1.0 - sigmoid_gate))
    up_grad = act_grad * gate_part * sigmoid_gate
    return jnp.concatenate([gate_grad, up_grad], axis=1).astype(jnp.bfloat16)

def blockwise(left_side, right_side, block_count):
    row_count, inner_width = left_side.shape
    block_width = inner_width // block_count
    left_blocks = left_side.astype(jnp.float32).reshape(row_count, block_count, block_width)
    right_blocks = right_side.astype(jnp.float32).reshape(block_count, block_width, right_side.shape[1])
    partial_value = jnp.einsum('rnk,nkf->nrf', left_blocks, right_blocks, precision=lax.Precision.HIGHEST)
    rounded = lax.optimization_barrier(partial_value.astype(jnp.bfloat16))
    return lax.optimization_barrier(jnp.sum(rounded.astype(jnp.float32), axis=0))

def expert_pass(packed):
    rows_in, cot_in, inner_weight, outer_weight = packed
    half_width = outer_weight.shape[0]
    contract_cols = (((1,), (1,)), ((), ()))
    contract_rows = (((0,), (0,)), ((), ()))
    hidden = blockwise(rows_in, inner_weight, N_DP)
    active = activate(hidden, half_width)
    expert_out = jnp.dot(active, outer_weight, preferred_element_type=jnp.float32).astype(jnp.bfloat16)
    act_grad = blockwise(cot_in, outer_weight.T, N_DP)
    hidden_cot = activate_grad(hidden, act_grad, half_width)
    output_grad = lax.dot_general(active, cot_in, contract_rows, preferred_element_type=jnp.float32).astype(jnp.bfloat16)
    hidden_grad = lax.dot_general(rows_in, hidden_cot, contract_rows, preferred_element_type=jnp.float32).astype(jnp.bfloat16)
    row_grad = lax.dot_general(hidden_cot, inner_weight, contract_cols, preferred_element_type=jnp.float32).astype(jnp.bfloat16)
    return (expert_out, row_grad, hidden_grad, output_grad)

def reference(tokens, cotangent, routing, gate_values, hidden_weight, output_weight):
    blocks = TOKENS // TOK_DEV
    highest = lax.Precision.HIGHEST
    tables = jax.vmap(lambda route_block, gate_block: slot_table(route_block, gate_block, EXPERTS, SLOTS))
    placed, gate_slot = tables(routing.reshape(blocks, TOK_DEV, TOP), gate_values.reshape(blocks, TOK_DEV, TOP))
    tok_blocks = tokens.reshape(blocks, TOK_DEV, D).astype(jnp.float32)
    cot_blocks = cotangent.reshape(blocks, TOK_DEV, D).astype(jnp.float32)
    token_rows = jnp.einsum('bst,btd->bsd', placed, tok_blocks, precision=highest).astype(jnp.bfloat16)
    scaled = (gate_slot[:, :, None] * jnp.einsum('bst,btd->bsd', placed, cot_blocks, precision=highest)).astype(jnp.bfloat16)

    def per_expert(values):
        return values.reshape(blocks, EXPERTS, SLOTS, D).transpose(1, 0, 2, 3).reshape(EXPERTS, blocks * SLOTS, D)

    def per_block(values):
        return values.reshape(EXPERTS, blocks, SLOTS, D).transpose(1, 0, 2, 3).reshape(blocks, EXPERTS * SLOTS, D)
    expert_out, row_grad, hidden_grad, output_grad = lax.map(expert_pass, (per_expert(token_rows), per_expert(scaled), hidden_weight, output_weight))
    weighted = placed * gate_slot[:, :, None]
    mixed = jnp.einsum('bst,bsd->btd', weighted, per_block(expert_out).astype(jnp.float32), precision=highest)
    token_grad = jnp.einsum('bst,bsd->btd', placed, per_block(row_grad).astype(jnp.float32), precision=highest)
    mixed = mixed.astype(jnp.bfloat16).reshape(TOKENS, D)
    token_grad = token_grad.astype(jnp.bfloat16).reshape(TOKENS, D)
    return (mixed, token_grad, hidden_grad, output_grad)
```

```python
import jax
import jax.numpy as jnp
from jax import lax
from jax.sharding import PartitionSpec as P

ROUTED = 256


def slot_table(routing_block, gate_block, expert_count, slot_count):
    tok_count = routing_block.shape[0]
    picked = routing_block.reshape(-1)
    onehot = (picked[:, None] == jnp.arange(expert_count, dtype=jnp.int32)[None, :]).astype(
        jnp.int32
    )
    earlier = jnp.cumsum(onehot, axis=0) - onehot
    ranking = jnp.sum(earlier * onehot, axis=1)
    slot_index = (picked * slot_count + ranking).reshape(tok_count, -1)
    target = jnp.arange(expert_count * slot_count, dtype=jnp.int32)
    matched = slot_index[None, :, :] == target[:, None, None]
    placed = jnp.any(matched, axis=2).astype(jnp.float32)
    gate_slot = jnp.sum(
        jnp.where(matched, gate_block[None, :, :], jnp.zeros_like(gate_block)[None, :, :]),
        axis=(1, 2),
    )
    return (placed, gate_slot)


def activate(hidden, half_width):
    gate_part = hidden[:, :half_width]
    up_part = hidden[:, half_width:]
    return (gate_part * jax.nn.sigmoid(gate_part) * up_part).astype(jnp.bfloat16)


def activate_grad(hidden, act_grad, half_width):
    gate_part = hidden[:, :half_width]
    up_part = hidden[:, half_width:]
    sigmoid_gate = jax.nn.sigmoid(gate_part)
    gate_grad = act_grad * up_part * sigmoid_gate * (1.0 + gate_part * (1.0 - sigmoid_gate))
    up_grad = act_grad * gate_part * sigmoid_gate
    return jnp.concatenate([gate_grad, up_grad], axis=1).astype(jnp.bfloat16)


def dp_sum(part):
    if lax.axis_size("dp") == 2:
        other = lax.ppermute(part, "dp", [(0, 1), (1, 0)])
        return part.astype(jnp.float32) + other.astype(jnp.float32)
    return lax.psum_scatter(part, "dp", scatter_dimension=0, tiled=True).astype(jnp.float32)


def dp_spread(rows):
    if lax.axis_size("dp") == 2:
        return rows
    return lax.all_gather(rows, "dp", axis=0, tiled=True)


def body(tokens, cotangent, routing, gate_values, hidden_weight, output_weight):
    tok_count, column_width = tokens.shape
    pick_count = routing.shape[1]
    expert_count = lax.axis_size("expert")
    slot_count = 2 * tok_count * pick_count // ROUTED
    row_total = expert_count * slot_count
    contract_cols = (((1,), (1,)), ((), ()))
    contract_rows = (((0,), (0,)), ((), ()))
    placed, gate_slot = slot_table(routing, gate_values, expert_count, slot_count)
    placed_half = placed.astype(jnp.bfloat16)
    send_shape = (expert_count, slot_count, column_width)
    token_rows = (
        jnp.dot(placed_half, tokens, preferred_element_type=jnp.float32)
        .astype(jnp.bfloat16)
        .reshape(send_shape)
    )
    cot_rows = (
        (gate_slot[:, None] * jnp.dot(placed_half, cotangent, preferred_element_type=jnp.float32))
        .astype(jnp.bfloat16)
        .reshape(send_shape)
    )
    inner_weight = hidden_weight[0]
    outer_weight = output_weight[0]
    half_width = outer_weight.shape[0]
    arrived = (
        lax.all_to_all(token_rows, "expert", split_axis=0, concat_axis=0, tiled=True),
        lax.all_to_all(cot_rows, "expert", split_axis=0, concat_axis=0, tiled=True),
    )
    expert_rows = arrived[0].reshape(row_total, column_width)
    scaled_cot = arrived[1].reshape(row_total, column_width)
    hidden_part = jnp.dot(
        expert_rows, inner_weight, preferred_element_type=jnp.float32
    ).astype(jnp.bfloat16)
    hidden = dp_sum(hidden_part)
    active = dp_spread(activate(hidden, half_width))
    expert_out = jnp.dot(active, outer_weight, preferred_element_type=jnp.float32).astype(
        jnp.bfloat16
    )
    expert_out, late_cot = lax.optimization_barrier((expert_out, scaled_cot))
    act_part = lax.dot_general(
        late_cot, outer_weight, contract_cols, preferred_element_type=jnp.float32
    ).astype(jnp.bfloat16)
    hidden_cot = dp_spread(activate_grad(hidden, dp_sum(act_part), half_width))
    output_grad = lax.dot_general(
        active, scaled_cot, contract_rows, preferred_element_type=jnp.float32
    ).astype(jnp.bfloat16)
    hidden_grad = lax.dot_general(
        expert_rows, hidden_cot, contract_rows, preferred_element_type=jnp.float32
    ).astype(jnp.bfloat16)
    row_grad = lax.dot_general(
        hidden_cot, inner_weight, contract_cols, preferred_element_type=jnp.float32
    ).astype(jnp.bfloat16)
    returned = (
        lax.all_to_all(
            expert_out.reshape(send_shape), "expert", split_axis=0, concat_axis=0, tiled=True
        ),
        lax.all_to_all(
            row_grad.reshape(send_shape), "expert", split_axis=0, concat_axis=0, tiled=True
        ),
    )
    back_out = returned[0]
    back_grad = returned[1]
    back_out = back_out.reshape(row_total, column_width)
    back_grad = back_grad.reshape(row_total, column_width)
    weighted = placed * gate_slot[:, None]
    mixed = lax.dot_general(
        weighted,
        back_out.astype(jnp.float32),
        contract_rows,
        precision=lax.Precision.HIGHEST,
        preferred_element_type=jnp.float32,
    ).astype(jnp.bfloat16)
    token_grad = lax.dot_general(
        placed_half, back_grad, contract_rows, preferred_element_type=jnp.float32
    ).astype(jnp.bfloat16)
    return (mixed, token_grad, hidden_grad[None], output_grad[None])


def solution(mesh):
    return jax.shard_map(
        body,
        mesh=mesh,
        in_specs=(
            P("expert", "dp"),
            P("expert", "dp"),
            P("expert", None),
            P("expert", None),
            P("expert", "dp", None),
            P("expert", None, "dp"),
        ),
        out_specs=(
            P("expert", "dp"),
            P("expert", "dp"),
            P("expert", "dp", None),
            P("expert", None, "dp"),
        ),
        check_vma=False,
    )
```

```python
import functools

import jax
import jax.numpy as jnp
from jax import lax
from jax.experimental import pallas as pl
from jax.experimental.pallas import tpu as pltpu
from jax.sharding import PartitionSpec as P


ROUTED = 256
VMEM_BYTES = 16 * 1024 * 1024


def slot_keys(route_ref, expert_ids):
    tok_count = route_ref.shape[1]
    chosen = route_ref[0:1, :] == expert_ids
    for k in range(1, route_ref.shape[0]):
        chosen = jnp.logical_or(chosen, route_ref[k : k + 1, :] == expert_ids)
    before = lax.broadcasted_iota(jnp.int32, (tok_count, tok_count), 0) < (
        lax.broadcasted_iota(jnp.int32, (tok_count, tok_count), 1)
    )
    rank = jnp.dot(
        chosen.astype(jnp.bfloat16), before.astype(jnp.bfloat16), preferred_element_type=jnp.float32
    )
    return jnp.where(chosen, rank.astype(jnp.int32), -1)


def expert_gates(route_ref, gate_ref, expert_ids):
    total = jnp.where(route_ref[0:1, :] == expert_ids, gate_ref[0:1, :], 0.0)
    for k in range(1, route_ref.shape[0]):
        total = total + jnp.where(route_ref[k : k + 1, :] == expert_ids, gate_ref[k : k + 1, :], 0.0)
    return total


def tile_width(width, limit):
    fits = [w for w in range(128, limit + 1, 128) if width % w == 0]
    return fits[-1] if fits else width


def experts_at(expert_count, tok_count, outer, own):
    at = lax.broadcasted_iota(jnp.int32, (expert_count, tok_count), 0)
    if outer > 1:
        shift = outer.bit_length() - 1
        at = (at & (outer - 1)) * (expert_count // outer) + lax.shift_right_logical(at, shift)
    return at ^ own


def gather_kernel(scaled, slot_count, outer, held, own_ref, route_ref, gate_ref, rows_ref, *refs):
    refs = refs[held:]
    out_refs, (placed_ref, gain_ref) = refs[:-2], refs[-2:]
    row_total, tok_count = placed_ref.shape
    expert_count, piece_rows = row_total // slot_count, out_refs[0].shape[0]

    @pl.when(pl.program_id(0) == 0)
    def _():
        expert_ids = experts_at(expert_count, tok_count, outer, own_ref[0])
        keys = slot_keys(route_ref, expert_ids)
        slots = lax.broadcasted_iota(jnp.int32, (slot_count, tok_count), 0)
        if scaled:
            gates = expert_gates(route_ref, gate_ref, expert_ids)
        for e in range(expert_count):
            here = pl.ds(e * slot_count, slot_count)
            matched = keys[e : e + 1, :] == slots
            placed_ref[here, :] = matched.astype(jnp.float32).astype(jnp.bfloat16)
            if scaled:
                gain_ref[here, :] = jnp.sum(
                    jnp.where(matched, gates[e : e + 1, :], 0.0), axis=1, keepdims=True
                )

    picked = jnp.dot(placed_ref[...], rows_ref[...], preferred_element_type=jnp.float32)
    if scaled:
        picked = gain_ref[...] * picked
    picked = picked.astype(jnp.bfloat16)
    for e, out_ref in enumerate(out_refs):
        out_ref[...] = picked[e * piece_rows : (e + 1) * piece_rows]


def gather_rows(own, routes, gates, rows, expert_count, slot_count, scaled, pieces, outer, held=()):
    tok_count, width = rows.shape
    row_total = expert_count * slot_count
    piece_rows = row_total // pieces
    block = tile_width(width, 1792)
    whole = pl.BlockSpec(routes.shape, lambda i: (0, 0))
    return pl.pallas_call(
        functools.partial(gather_kernel, scaled, slot_count, outer, len(held)),
        grid=(width // block,),
        in_specs=[
            pl.BlockSpec(memory_space=pltpu.SMEM),
            whole,
            whole,
            pl.BlockSpec((tok_count, block), lambda i: (0, i)),
        ]
        + [pl.BlockSpec(memory_space=pl.ANY)] * len(held),
        out_specs=[pl.BlockSpec((piece_rows, block), lambda i: (0, i))] * pieces,
        out_shape=[jax.ShapeDtypeStruct((piece_rows, width), jnp.bfloat16)] * pieces,
        scratch_shapes=[
            pltpu.VMEM((row_total, tok_count), jnp.bfloat16),
            pltpu.VMEM((row_total, 1), jnp.float32),
        ],
        compiler_params=pltpu.CompilerParams(vmem_limit_bytes=VMEM_BYTES if held else None),
        cost_estimate=pl.CostEstimate(
            flops=2 * row_total * tok_count * width,
            bytes_accessed=2 * (tok_count + row_total) * width,
            transcendentals=0,
        ),
    )(own, routes, gates, rows, *held)


def combine_kernel(weighted, expert_count, outer, own_ref, route_ref, gate_ref, *refs):
    row_refs, (out_ref, weight_ref) = refs[:-2], refs[-2:]
    row_total, tok_count = weight_ref.shape[-2:]
    slot_count = row_total // expert_count

    @pl.when(pl.program_id(0) == 0)
    def _():
        expert_ids = experts_at(expert_count, tok_count, outer, own_ref[0])
        keys = slot_keys(route_ref, expert_ids)
        slots = lax.broadcasted_iota(jnp.int32, (slot_count, tok_count), 0)
        if weighted:
            gates = expert_gates(route_ref, gate_ref, expert_ids)
        for e in range(expert_count):
            here = pl.ds(e * slot_count, slot_count)
            matched = keys[e : e + 1, :] == slots
            if not weighted:
                weight_ref[0, here, :] = matched.astype(jnp.float32).astype(jnp.bfloat16)
                continue
            left = jnp.where(matched, gates[e : e + 1, :], 0.0)
            for part in range(weight_ref.shape[0]):
                term = left.astype(jnp.bfloat16)
                weight_ref[part, here, :] = term
                left = left - term.astype(jnp.float32)

    rows = jnp.concatenate([ref[...] for ref in row_refs]) if row_refs[1:] else row_refs[0][...]
    total = None
    for part in range(weight_ref.shape[0]):
        term = lax.dot_general(
            weight_ref[part], rows, (((0,), (0,)), ((), ())), preferred_element_type=jnp.float32
        )
        total = term if total is None else total + term
    out_ref[...] = total.astype(jnp.bfloat16)


def combine_rows(own, routes, gates, pieces, expert_count, weighted, outer):
    tok_count = routes.shape[1]
    row_total, width = sum(piece.shape[0] for piece in pieces), pieces[0].shape[1]
    block = tile_width(width, 896)
    whole = pl.BlockSpec(routes.shape, lambda i: (0, 0))
    parts = 3 if weighted else 1
    return pl.pallas_call(
        functools.partial(combine_kernel, weighted, expert_count, outer),
        grid=(width // block,),
        in_specs=[pl.BlockSpec(memory_space=pltpu.SMEM), whole, whole]
        + [pl.BlockSpec((piece.shape[0], block), lambda i: (0, i)) for piece in pieces],
        out_specs=pl.BlockSpec((tok_count, block), lambda i: (0, i)),
        out_shape=jax.ShapeDtypeStruct((tok_count, width), jnp.bfloat16),
        scratch_shapes=[pltpu.VMEM((parts, row_total, tok_count), jnp.bfloat16)],
        compiler_params=pltpu.CompilerParams(vmem_limit_bytes=VMEM_BYTES),
        cost_estimate=pl.CostEstimate(
            flops=2 * parts * row_total * tok_count * width,
            bytes_accessed=2 * (tok_count + row_total) * width,
            transcendentals=0,
        ),
    )(own, routes, gates, *pieces)


def activate(hidden, half_width):
    gate_part = hidden[:, :half_width]
    up_part = hidden[:, half_width:]
    return (gate_part * jax.nn.sigmoid(gate_part) * up_part).astype(jnp.bfloat16)


def activate_grad(hidden, act_grad, half_width):
    gate_part = hidden[:, :half_width]
    up_part = hidden[:, half_width:]
    sigmoid_gate = jax.nn.sigmoid(gate_part)
    gate_grad = act_grad * up_part * sigmoid_gate * (1.0 + gate_part * (1.0 - sigmoid_gate))
    up_grad = act_grad * gate_part * sigmoid_gate
    return jnp.concatenate([gate_grad, up_grad], axis=1).astype(jnp.bfloat16)


def hold_kernel(count, *refs):
    copies = [
        pltpu.make_async_copy(refs[k], refs[count + k], refs[2 * count].at[k]) for k in range(count)
    ]
    for copy in copies:
        copy.start()
    for copy in copies:
        copy.wait()


def hold(*arrays):
    count = len(arrays)
    return pl.pallas_call(
        functools.partial(hold_kernel, count),
        in_specs=[pl.BlockSpec(memory_space=pl.ANY)] * count,
        out_specs=[pl.BlockSpec(memory_space=pltpu.VMEM)] * count,
        out_shape=[pltpu.VMEM(a.shape, a.dtype) for a in arrays],
        scratch_shapes=[pltpu.SemaphoreType.DMA((count,))],
        compiler_params=pltpu.CompilerParams(vmem_limit_bytes=VMEM_BYTES),
        cost_estimate=pl.CostEstimate(
            flops=0, bytes_accessed=4 * sum(a.size for a in arrays), transcendentals=0
        ),
    )(*arrays)


def column_kernel(first, left_ref, right_ref, out_ref):
    width = out_ref.shape[1]
    out_ref[...] = jnp.dot(
        left_ref[...], right_ref[:, first : first + width], preferred_element_type=jnp.float32
    ).astype(jnp.bfloat16)


def part_product(kernel, left, right, first, width):
    row_total, depth = left.shape
    return pl.pallas_call(
        functools.partial(kernel, first),
        in_specs=[pl.BlockSpec(memory_space=pltpu.VMEM)] * 2,
        out_specs=pl.BlockSpec(memory_space=pltpu.VMEM),
        out_shape=jax.ShapeDtypeStruct((row_total, width), jnp.bfloat16),
        compiler_params=pltpu.CompilerParams(vmem_limit_bytes=VMEM_BYTES),
        cost_estimate=pl.CostEstimate(
            flops=2 * row_total * depth * width,
            bytes_accessed=2 * (row_total + width) * depth + 2 * row_total * width,
            transcendentals=0,
        ),
    )(left, right)


def held_kernel(right_dim, block, groups, left_ref, right_ref, *out_refs):
    here = pl.ds(pl.multiple_of(pl.program_id(0) * block, block), block)
    right = right_ref[here, :] if right_dim == 1 else right_ref[:, here]
    rows = lax.dot_general(
        left_ref[...], right, (((1,), (right_dim,)), ((), ())), preferred_element_type=jnp.float32
    ).astype(jnp.bfloat16)
    run = rows.shape[0] // (len(out_refs) * groups)
    for p, out_ref in enumerate(out_refs):
        for g in range(groups):
            first = (g * len(out_refs) + p) * run
            out_ref[g * run : (g + 1) * run, :] = rows[first : first + run]


def held_product(left, right, right_dim, limit, pieces, groups):
    row_total, depth = left.shape
    width = right.shape[1 - right_dim]
    block = tile_width(width, limit)
    piece_rows = row_total // pieces
    return pl.pallas_call(
        functools.partial(held_kernel, right_dim, block, groups),
        grid=(width // block,),
        in_specs=[
            pl.BlockSpec((row_total, depth), lambda i: (0, 0)),
            pl.BlockSpec(memory_space=pltpu.VMEM),
        ],
        out_specs=[pl.BlockSpec((piece_rows, block), lambda i: (0, i))] * pieces,
        out_shape=[jax.ShapeDtypeStruct((piece_rows, width), jnp.bfloat16)] * pieces,
        compiler_params=pltpu.CompilerParams(vmem_limit_bytes=VMEM_BYTES),
        cost_estimate=pl.CostEstimate(
            flops=2 * row_total * depth * width,
            bytes_accessed=2 * (row_total + width) * depth + 2 * row_total * width,
            transcendentals=0,
        ),
    )(left, right)


def cot_kernel(first, left_ref, right_ref, out_ref):
    width = out_ref.shape[1]
    out_ref[...] = lax.dot_general(
        left_ref[...],
        right_ref[first : first + width, :],
        (((1,), (1,)), ((), ())),
        preferred_element_type=jnp.float32,
    ).astype(jnp.bfloat16)


def trade(pieces, step):
    count = lax.axis_size("expert")
    got = list(pieces)
    for k in range(len(pieces) - 1, 0, -1):
        pairs = [(i, i ^ (k * step)) for i in range(count)]
        got[k] = lax.ppermute(pieces[k], "expert", pairs)
    return got


def regroup(pieces, parts):
    rows = pieces[0].shape[0] // parts
    return [jnp.concatenate([p[k * rows : (k + 1) * rows] for p in pieces]) for k in range(parts)]


def cut(rows, parts):
    size = rows.shape[0] // parts
    return [rows[k * size : (k + 1) * size] for k in range(parts)]


def send_back(out_pieces, inner):
    return trade(regroup(trade(out_pieces, inner), inner), 1)


def dp_swap(part):
    return lax.ppermute(part, "dp", [(0, 1), (1, 0)])


def dp_sum(part):
    return lax.psum_scatter(part, "dp", scatter_dimension=0, tiled=True).astype(jnp.float32)


def pair_sum(pairs):
    sums = [own.astype(jnp.float32) + other.astype(jnp.float32) for own, other in pairs]
    return sums[0] if len(sums) == 1 else jnp.concatenate(sums, axis=1)


def dp_spread(rows):
    if lax.axis_size("dp") == 2:
        return rows
    return lax.all_gather(rows, "dp", axis=0, tiled=True)


def middle_ring(expert_rows, scaled_cot, inner_weight, outer_weight, outer, inner):
    contract_cols = (((1,), (1,)), ((), ()))
    half_width = outer_weight.shape[0]
    part = jnp.dot(jnp.concatenate(expert_rows), inner_weight, preferred_element_type=jnp.float32)
    hidden = dp_sum(part.astype(jnp.bfloat16))
    active = dp_spread(activate(hidden, half_width))
    expert_out = jnp.dot(active, outer_weight, preferred_element_type=jnp.float32)
    out_pieces = cut(expert_out.astype(jnp.bfloat16), outer)
    back_out = send_back(out_pieces, inner)
    part = lax.dot_general(
        scaled_cot, outer_weight, contract_cols, preferred_element_type=jnp.float32
    )
    act_grad = dp_sum(part.astype(jnp.bfloat16))
    hidden_cot = dp_spread(activate_grad(hidden, act_grad, half_width))
    row_grad = lax.dot_general(
        hidden_cot, inner_weight, contract_cols, preferred_element_type=jnp.float32
    )
    grad_pieces = regroup(cut(row_grad.astype(jnp.bfloat16), outer), inner)
    return active, hidden_cot, back_out, grad_pieces


def middle_pair(expert_rows, scaled_cot, inner_weight, outer_weight, outer, inner):
    half_width = outer_weight.shape[0]
    inner_weight, outer_weight = hold(inner_weight, outer_weight)
    sides, actives, out_pieces = [], [], []
    for at, rows in enumerate(expert_rows):
        sides.append([])
        for side in range(2):
            part = part_product(column_kernel, rows, inner_weight, side * half_width, half_width)
            sides[at].append((part, dp_swap(part)))
    for at, side in enumerate(sides):
        actives.append(activate(pair_sum(side), half_width))
        out_pieces += held_product(actives[at], outer_weight, 0, 512, outer // 2, 1)
    active = jnp.concatenate(actives)
    own_piece, late_sides = lax.optimization_barrier((out_pieces[0], sides))
    back_out = send_back([own_piece, *out_pieces[1:]], inner)

    chunk = half_width // CHUNKS
    pairs = []
    for at in range(CHUNKS):
        part = part_product(cot_kernel, scaled_cot, outer_weight, at * chunk, chunk)
        pairs.append((part, dp_swap(part)))
    hidden = jnp.concatenate([pair_sum(side) for side in late_sides])
    hidden_cot = activate_grad(hidden, pair_sum(pairs), half_width)
    grad_pieces = held_product(hidden_cot, inner_weight, 1, 512, inner, outer)
    return active, hidden_cot, back_out, grad_pieces


def body(tokens, cotangent, routing, gate_values, hidden_weight, output_weight):
    tok_count, _ = tokens.shape
    pick_count = routing.shape[1]
    expert_count = lax.axis_size("expert")
    slot_count = 2 * tok_count * pick_count // ROUTED
    contract_rows = (((0,), (0,)), ((), ()))
    outer = 1 << ((expert_count.bit_length() - 1) // 2)
    inner = expert_count // outer
    own = lax.axis_index("expert").astype(jnp.int32)
    routes, gates = routing.T, gate_values.T
    inner_weight = hidden_weight[0]
    outer_weight = output_weight[0]
    table = (routes, gates)

    mine = own[None]
    token_pieces = gather_rows(
        mine, *table, tokens, expert_count, slot_count, False, outer, 1
    )
    moved = trade(token_pieces, inner)
    expert_rows = []
    for run in (moved[: outer // 2], moved[outer // 2 :]):
        run = regroup(run, inner)
        run = trade(run, 1)
        expert_rows.append(jnp.concatenate(regroup(run, outer // 2)))

    cot = gather_rows(mine, *table, cotangent, expert_count, slot_count, True, inner, outer)
    cot = trade(cot, 1)
    cot = regroup(cot, outer)
    scaled_cot = jnp.concatenate(trade(cot, inner))

    middle = middle_pair if lax.axis_size("dp") == 2 else middle_ring
    active, hidden_cot, back_out, grad_pieces = middle(
        expert_rows, scaled_cot, inner_weight, outer_weight, outer, inner
    )
    grad_pieces = trade(grad_pieces, 1)
    grad_pieces = regroup(grad_pieces, outer)
    back_grad = trade(grad_pieces, inner)

    output_grad = lax.dot_general(
        active, scaled_cot, contract_rows, preferred_element_type=jnp.float32
    ).astype(jnp.bfloat16)
    hidden_grad = lax.dot_general(
        jnp.concatenate(expert_rows), hidden_cot, contract_rows, preferred_element_type=jnp.float32
    ).astype(jnp.bfloat16)
    mixed = combine_rows(mine, *table, back_out, expert_count, True, outer)
    token_grad = combine_rows(mine, *table, back_grad, expert_count, False, 1)
    return (mixed, token_grad, hidden_grad[None], output_grad[None])


CHUNKS = 2


def solution(mesh):
    return jax.shard_map(
        body,
        mesh=mesh,
        in_specs=(
            P("expert", "dp"),
            P("expert", "dp"),
            P("expert", None),
            P("expert", None),
            P("expert", "dp", None),
            P("expert", None, "dp"),
        ),
        out_specs=(
            P("expert", "dp"),
            P("expert", "dp"),
            P("expert", "dp", None),
            P("expert", None, "dp"),
        ),
        check_vma=False,
    )
```

```python
import functools

import jax
import jax.numpy as jnp
from jax import lax
from jax.experimental import pallas as pl
from jax.experimental.pallas import tpu as pltpu
from jax.sharding import PartitionSpec as P


ROUTED = 256
VMEM_BYTES = 16 * 1024 * 1024


def slot_keys(route_ref, expert_ids):
    tok_count = route_ref.shape[1]
    chosen = route_ref[0:1, :] == expert_ids
    for k in range(1, route_ref.shape[0]):
        chosen = jnp.logical_or(chosen, route_ref[k : k + 1, :] == expert_ids)
    before = lax.broadcasted_iota(jnp.int32, (tok_count, tok_count), 0) < (
        lax.broadcasted_iota(jnp.int32, (tok_count, tok_count), 1)
    )
    rank = jnp.dot(
        chosen.astype(jnp.bfloat16), before.astype(jnp.bfloat16), preferred_element_type=jnp.float32
    )
    return jnp.where(chosen, rank.astype(jnp.int32), -1)


def expert_gates(route_ref, gate_ref, expert_ids):
    total = jnp.where(route_ref[0:1, :] == expert_ids, gate_ref[0:1, :], 0.0)
    for k in range(1, route_ref.shape[0]):
        total = total + jnp.where(route_ref[k : k + 1, :] == expert_ids, gate_ref[k : k + 1, :], 0.0)
    return total


def tile_width(width, limit):
    fits = [w for w in range(128, limit + 1, 128) if width % w == 0]
    return fits[-1] if fits else width


def experts_at(expert_count, tok_count, outer, own):
    at = lax.broadcasted_iota(jnp.int32, (expert_count, tok_count), 0)
    if outer > 1:
        shift = outer.bit_length() - 1
        at = (at & (outer - 1)) * (expert_count // outer) + lax.shift_right_logical(at, shift)
    return at ^ own


def gather_kernel(scaled, slot_count, outer, held, own_ref, route_ref, gate_ref, rows_ref, *refs):
    refs = refs[held:]
    out_refs, (placed_ref, gain_ref) = refs[:-2], refs[-2:]
    row_total, tok_count = placed_ref.shape
    expert_count, piece_rows = row_total // slot_count, out_refs[0].shape[0]

    @pl.when(pl.program_id(0) == 0)
    def _():
        expert_ids = experts_at(expert_count, tok_count, outer, own_ref[0])
        keys = slot_keys(route_ref, expert_ids)
        slots = lax.broadcasted_iota(jnp.int32, (slot_count, tok_count), 0)
        if scaled:
            gates = expert_gates(route_ref, gate_ref, expert_ids)
        for e in range(expert_count):
            here = pl.ds(e * slot_count, slot_count)
            matched = keys[e : e + 1, :] == slots
            placed_ref[here, :] = matched.astype(jnp.float32).astype(jnp.bfloat16)
            if scaled:
                gain_ref[here, :] = jnp.sum(
                    jnp.where(matched, gates[e : e + 1, :], 0.0), axis=1, keepdims=True
                )

    picked = jnp.dot(placed_ref[...], rows_ref[...], preferred_element_type=jnp.float32)
    if scaled:
        picked = gain_ref[...] * picked
    picked = picked.astype(jnp.bfloat16)
    for e, out_ref in enumerate(out_refs):
        out_ref[...] = picked[e * piece_rows : (e + 1) * piece_rows]


def gather_rows(own, routes, gates, rows, expert_count, slot_count, scaled, pieces, outer, held=()):
    tok_count, width = rows.shape
    row_total = expert_count * slot_count
    piece_rows = row_total // pieces
    block = tile_width(width, 1792)
    whole = pl.BlockSpec(routes.shape, lambda i: (0, 0))
    return pl.pallas_call(
        functools.partial(gather_kernel, scaled, slot_count, outer, len(held)),
        grid=(width // block,),
        in_specs=[
            pl.BlockSpec(memory_space=pltpu.SMEM),
            whole,
            whole,
            pl.BlockSpec((tok_count, block), lambda i: (0, i)),
        ]
        + [pl.BlockSpec(memory_space=pl.ANY)] * len(held),
        out_specs=[pl.BlockSpec((piece_rows, block), lambda i: (0, i))] * pieces,
        out_shape=[jax.ShapeDtypeStruct((piece_rows, width), jnp.bfloat16)] * pieces,
        scratch_shapes=[
            pltpu.VMEM((row_total, tok_count), jnp.bfloat16),
            pltpu.VMEM((row_total, 1), jnp.float32),
        ],
        compiler_params=pltpu.CompilerParams(vmem_limit_bytes=VMEM_BYTES if held else None),
        cost_estimate=pl.CostEstimate(
            flops=2 * row_total * tok_count * width,
            bytes_accessed=2 * (tok_count + row_total) * width,
            transcendentals=0,
        ),
    )(own, routes, gates, rows, *held)


def combine_kernel(weighted, expert_count, outer, own_ref, route_ref, gate_ref, *refs):
    row_refs, (out_ref, weight_ref) = refs[:-2], refs[-2:]
    row_total, tok_count = weight_ref.shape[-2:]
    slot_count = row_total // expert_count

    @pl.when(pl.program_id(0) == 0)
    def _():
        expert_ids = experts_at(expert_count, tok_count, outer, own_ref[0])
        keys = slot_keys(route_ref, expert_ids)
        slots = lax.broadcasted_iota(jnp.int32, (slot_count, tok_count), 0)
        if weighted:
            gates = expert_gates(route_ref, gate_ref, expert_ids)
        for e in range(expert_count):
            here = pl.ds(e * slot_count, slot_count)
            matched = keys[e : e + 1, :] == slots
            if not weighted:
                weight_ref[0, here, :] = matched.astype(jnp.float32).astype(jnp.bfloat16)
                continue
            left = jnp.where(matched, gates[e : e + 1, :], 0.0)
            for part in range(weight_ref.shape[0]):
                term = left.astype(jnp.bfloat16)
                weight_ref[part, here, :] = term
                left = left - term.astype(jnp.float32)

    rows = jnp.concatenate([ref[...] for ref in row_refs]) if row_refs[1:] else row_refs[0][...]
    total = None
    for part in range(weight_ref.shape[0]):
        term = lax.dot_general(
            weight_ref[part], rows, (((0,), (0,)), ((), ())), preferred_element_type=jnp.float32
        )
        total = term if total is None else total + term
    out_ref[...] = total.astype(jnp.bfloat16)


def combine_rows(own, routes, gates, pieces, expert_count, weighted, outer):
    tok_count = routes.shape[1]
    row_total, width = sum(piece.shape[0] for piece in pieces), pieces[0].shape[1]
    block = tile_width(width, 896)
    whole = pl.BlockSpec(routes.shape, lambda i: (0, 0))
    parts = 3 if weighted else 1
    return pl.pallas_call(
        functools.partial(combine_kernel, weighted, expert_count, outer),
        grid=(width // block,),
        in_specs=[pl.BlockSpec(memory_space=pltpu.SMEM), whole, whole]
        + [pl.BlockSpec((piece.shape[0], block), lambda i: (0, i)) for piece in pieces],
        out_specs=pl.BlockSpec((tok_count, block), lambda i: (0, i)),
        out_shape=jax.ShapeDtypeStruct((tok_count, width), jnp.bfloat16),
        scratch_shapes=[pltpu.VMEM((parts, row_total, tok_count), jnp.bfloat16)],
        compiler_params=pltpu.CompilerParams(vmem_limit_bytes=VMEM_BYTES),
        cost_estimate=pl.CostEstimate(
            flops=2 * parts * row_total * tok_count * width,
            bytes_accessed=2 * (tok_count + row_total) * width,
            transcendentals=0,
        ),
    )(own, routes, gates, *pieces)


def activate(hidden, half_width):
    gate_part = hidden[:, :half_width]
    up_part = hidden[:, half_width:]
    return (gate_part * jax.nn.sigmoid(gate_part) * up_part).astype(jnp.bfloat16)


def activate_grad(hidden, act_grad, half_width):
    gate_part = hidden[:, :half_width]
    up_part = hidden[:, half_width:]
    sigmoid_gate = jax.nn.sigmoid(gate_part)
    gate_grad = act_grad * up_part * sigmoid_gate * (1.0 + gate_part * (1.0 - sigmoid_gate))
    up_grad = act_grad * gate_part * sigmoid_gate
    return jnp.concatenate([gate_grad, up_grad], axis=1).astype(jnp.bfloat16)


def hold_kernel(count, *refs):
    copies = [
        pltpu.make_async_copy(refs[k], refs[count + k], refs[2 * count].at[k]) for k in range(count)
    ]
    for copy in copies:
        copy.start()
    for copy in copies:
        copy.wait()


def hold(*arrays):
    count = len(arrays)
    return pl.pallas_call(
        functools.partial(hold_kernel, count),
        in_specs=[pl.BlockSpec(memory_space=pl.ANY)] * count,
        out_specs=[pl.BlockSpec(memory_space=pltpu.VMEM)] * count,
        out_shape=[pltpu.VMEM(a.shape, a.dtype) for a in arrays],
        scratch_shapes=[pltpu.SemaphoreType.DMA((count,))],
        compiler_params=pltpu.CompilerParams(vmem_limit_bytes=VMEM_BYTES),
        cost_estimate=pl.CostEstimate(
            flops=0, bytes_accessed=4 * sum(a.size for a in arrays), transcendentals=0
        ),
    )(*arrays)


def column_kernel(first, left_ref, right_ref, out_ref):
    width = out_ref.shape[1]
    out_ref[...] = jnp.dot(
        left_ref[...], right_ref[:, first : first + width], preferred_element_type=jnp.float32
    ).astype(jnp.bfloat16)


def part_product(kernel, left, right, first, width):
    row_total, depth = left.shape
    return pl.pallas_call(
        functools.partial(kernel, first),
        in_specs=[pl.BlockSpec(memory_space=pltpu.VMEM)] * 2,
        out_specs=pl.BlockSpec(memory_space=pltpu.VMEM),
        out_shape=jax.ShapeDtypeStruct((row_total, width), jnp.bfloat16),
        compiler_params=pltpu.CompilerParams(vmem_limit_bytes=VMEM_BYTES),
        cost_estimate=pl.CostEstimate(
            flops=2 * row_total * depth * width,
            bytes_accessed=2 * (row_total + width) * depth + 2 * row_total * width,
            transcendentals=0,
        ),
    )(left, right)


def held_kernel(right_dim, block, groups, left_ref, right_ref, *out_refs):
    here = pl.ds(pl.multiple_of(pl.program_id(0) * block, block), block)
    right = right_ref[here, :] if right_dim == 1 else right_ref[:, here]
    rows = lax.dot_general(
        left_ref[...], right, (((1,), (right_dim,)), ((), ())), preferred_element_type=jnp.float32
    ).astype(jnp.bfloat16)
    run = rows.shape[0] // (len(out_refs) * groups)
    for p, out_ref in enumerate(out_refs):
        for g in range(groups):
            first = (g * len(out_refs) + p) * run
            out_ref[g * run : (g + 1) * run, :] = rows[first : first + run]


def held_product(left, right, right_dim, limit, pieces, groups):
    row_total, depth = left.shape
    width = right.shape[1 - right_dim]
    block = tile_width(width, limit)
    piece_rows = row_total // pieces
    return pl.pallas_call(
        functools.partial(held_kernel, right_dim, block, groups),
        grid=(width // block,),
        in_specs=[
            pl.BlockSpec((row_total, depth), lambda i: (0, 0)),
            pl.BlockSpec(memory_space=pltpu.VMEM),
        ],
        out_specs=[pl.BlockSpec((piece_rows, block), lambda i: (0, i))] * pieces,
        out_shape=[jax.ShapeDtypeStruct((piece_rows, width), jnp.bfloat16)] * pieces,
        compiler_params=pltpu.CompilerParams(vmem_limit_bytes=VMEM_BYTES),
        cost_estimate=pl.CostEstimate(
            flops=2 * row_total * depth * width,
            bytes_accessed=2 * (row_total + width) * depth + 2 * row_total * width,
            transcendentals=0,
        ),
    )(left, right)


def cot_kernel(first, left_ref, right_ref, out_ref):
    width = out_ref.shape[1]
    out_ref[...] = lax.dot_general(
        left_ref[...],
        right_ref[first : first + width, :],
        (((1,), (1,)), ((), ())),
        preferred_element_type=jnp.float32,
    ).astype(jnp.bfloat16)


def trade(pieces, step):
    count = lax.axis_size("expert")
    got = list(pieces)
    for k in range(len(pieces) - 1, 0, -1):
        pairs = [(i, i ^ (k * step)) for i in range(count)]
        got[k] = lax.ppermute(pieces[k], "expert", pairs)
    return got


def regroup(pieces, parts):
    rows = pieces[0].shape[0] // parts
    return [jnp.concatenate([p[k * rows : (k + 1) * rows] for p in pieces]) for k in range(parts)]


def cut(rows, parts):
    size = rows.shape[0] // parts
    return [rows[k * size : (k + 1) * size] for k in range(parts)]


def send_back(out_pieces, inner):
    return trade(regroup(trade(out_pieces, inner), inner), 1)


def dp_swap(part):
    return lax.ppermute(part, "dp", [(0, 1), (1, 0)])


def dp_sum(part):
    return lax.psum_scatter(part, "dp", scatter_dimension=0, tiled=True).astype(jnp.float32)


def pair_sum(pairs):
    sums = [own.astype(jnp.float32) + other.astype(jnp.float32) for own, other in pairs]
    return sums[0] if len(sums) == 1 else jnp.concatenate(sums, axis=1)


def dp_spread(rows):
    if lax.axis_size("dp") == 2:
        return rows
    return lax.all_gather(rows, "dp", axis=0, tiled=True)


def middle_ring(expert_rows, scaled_cot, inner_weight, outer_weight, outer, inner):
    contract_cols = (((1,), (1,)), ((), ()))
    half_width = outer_weight.shape[0]
    part = jnp.dot(jnp.concatenate(expert_rows), inner_weight, preferred_element_type=jnp.float32)
    hidden = dp_sum(part.astype(jnp.bfloat16))
    active = dp_spread(activate(hidden, half_width))
    expert_out = jnp.dot(active, outer_weight, preferred_element_type=jnp.float32)
    out_pieces = cut(expert_out.astype(jnp.bfloat16), outer)
    back_out = send_back(out_pieces, inner)
    part = lax.dot_general(
        scaled_cot, outer_weight, contract_cols, preferred_element_type=jnp.float32
    )
    act_grad = dp_sum(part.astype(jnp.bfloat16))
    hidden_cot = dp_spread(activate_grad(hidden, act_grad, half_width))
    row_grad = lax.dot_general(
        hidden_cot, inner_weight, contract_cols, preferred_element_type=jnp.float32
    )
    grad_pieces = regroup(cut(row_grad.astype(jnp.bfloat16), outer), inner)
    return active, hidden_cot, back_out, grad_pieces


def middle_pair(expert_rows, scaled_cot, inner_weight, outer_weight, outer, inner):
    half_width = outer_weight.shape[0]
    inner_weight, outer_weight = hold(inner_weight, outer_weight)
    sides, actives, out_pieces = [], [], []
    for at, rows in enumerate(expert_rows):
        sides.append([])
        for side in range(2):
            part = part_product(column_kernel, rows, inner_weight, side * half_width, half_width)
            sides[at].append((part, dp_swap(part)))
    for at, side in enumerate(sides):
        actives.append(activate(pair_sum(side), half_width))
        out_pieces += held_product(actives[at], outer_weight, 0, 512, outer // 2, 1)
    active = jnp.concatenate(actives)
    own_piece, late_sides = lax.optimization_barrier((out_pieces[0], sides))
    back_out = send_back([own_piece, *out_pieces[1:]], inner)

    chunk = half_width // CHUNKS
    pairs = []
    for at in range(CHUNKS):
        part = part_product(cot_kernel, scaled_cot, outer_weight, at * chunk, chunk)
        pairs.append((part, dp_swap(part)))
    hidden = jnp.concatenate([pair_sum(side) for side in late_sides])
    hidden_cot = activate_grad(hidden, pair_sum(pairs), half_width)
    grad_pieces = held_product(hidden_cot, inner_weight, 1, 512, inner, outer)
    return active, hidden_cot, back_out, grad_pieces


def body(tokens, cotangent, routing, gate_values, hidden_weight, output_weight):
    tok_count, _ = tokens.shape
    pick_count = routing.shape[1]
    expert_count = lax.axis_size("expert")
    slot_count = 2 * tok_count * pick_count // ROUTED
    contract_rows = (((0,), (0,)), ((), ()))
    outer = 1 << ((expert_count.bit_length() - 1) // 2)
    inner = expert_count // outer
    own = lax.axis_index("expert").astype(jnp.int32)
    routes, gates = routing.T, gate_values.T
    inner_weight = hidden_weight[0]
    outer_weight = output_weight[0]
    table = (routes, gates)

    mine = own[None]
    token_pieces = gather_rows(
        mine, *table, tokens, expert_count, slot_count, False, outer, 1
    )
    moved = trade(token_pieces, inner)
    expert_rows = []
    for run in (moved[: outer // 2], moved[outer // 2 :]):
        run = regroup(run, inner)
        run = trade(run, 1)
        expert_rows.append(jnp.concatenate(regroup(run, outer // 2)))

    cot = gather_rows(mine, *table, cotangent, expert_count, slot_count, True, inner, outer)
    cot = trade(cot, 1)
    cot = regroup(cot, outer)
    scaled_cot = jnp.concatenate(trade(cot, inner))

    middle = middle_pair if lax.axis_size("dp") == 2 else middle_ring
    active, hidden_cot, back_out, grad_pieces = middle(
        expert_rows, scaled_cot, inner_weight, outer_weight, outer, inner
    )
    grad_pieces = trade(grad_pieces, 1)
    runs = []
    for part in (grad_pieces[: inner // 2], grad_pieces[inner // 2 :]):
        part = regroup(part, outer)
        runs.append(trade(part, inner))
    back_grad = [run[k] for k in range(outer) for run in runs]

    output_grad = lax.dot_general(
        active, scaled_cot, contract_rows, preferred_element_type=jnp.float32
    ).astype(jnp.bfloat16)
    hidden_grad = lax.dot_general(
        jnp.concatenate(expert_rows), hidden_cot, contract_rows, preferred_element_type=jnp.float32
    ).astype(jnp.bfloat16)
    mixed = combine_rows(mine, *table, back_out, expert_count, True, outer)
    token_grad = combine_rows(mine, *table, back_grad, expert_count, False, 1)
    return (mixed, token_grad, hidden_grad[None], output_grad[None])


CHUNKS = 2


def solution(mesh):
    return jax.shard_map(
        body,
        mesh=mesh,
        in_specs=(
            P("expert", "dp"),
            P("expert", "dp"),
            P("expert", None),
            P("expert", None),
            P("expert", "dp", None),
            P("expert", None, "dp"),
        ),
        out_specs=(
            P("expert", "dp"),
            P("expert", "dp"),
            P("expert", "dp", None),
            P("expert", None, "dp"),
        ),
        check_vma=False,
    )
```

```python
import functools

import jax
import jax.numpy as jnp
from jax import lax
from jax.experimental import pallas as pl
from jax.experimental.pallas import tpu as pltpu
from jax.sharding import PartitionSpec as P


ROUTED = 256
VMEM_BYTES = 16 * 1024 * 1024


def slot_keys(route_ref, expert_ids):
    tok_count = route_ref.shape[1]
    chosen = route_ref[0:1, :] == expert_ids
    for k in range(1, route_ref.shape[0]):
        chosen = jnp.logical_or(chosen, route_ref[k : k + 1, :] == expert_ids)
    before = lax.broadcasted_iota(jnp.int32, (tok_count, tok_count), 0) < (
        lax.broadcasted_iota(jnp.int32, (tok_count, tok_count), 1)
    )
    rank = jnp.dot(
        chosen.astype(jnp.bfloat16), before.astype(jnp.bfloat16), preferred_element_type=jnp.float32
    )
    return jnp.where(chosen, rank.astype(jnp.int32), -1)


def expert_gates(route_ref, gate_ref, expert_ids):
    total = jnp.where(route_ref[0:1, :] == expert_ids, gate_ref[0:1, :], 0.0)
    for k in range(1, route_ref.shape[0]):
        total = total + jnp.where(route_ref[k : k + 1, :] == expert_ids, gate_ref[k : k + 1, :], 0.0)
    return total


def tile_width(width, limit):
    fits = [w for w in range(128, limit + 1, 128) if width % w == 0]
    return fits[-1] if fits else width


def experts_at(expert_count, tok_count, outer, own):
    at = lax.broadcasted_iota(jnp.int32, (expert_count, tok_count), 0)
    if outer > 1:
        shift = outer.bit_length() - 1
        at = (at & (outer - 1)) * (expert_count // outer) + lax.shift_right_logical(at, shift)
    return at ^ own


def gather_kernel(scaled, slot_count, outer, held, own_ref, route_ref, gate_ref, rows_ref, *refs):
    refs = refs[held:]
    out_refs, (table_ref, placed_ref, gain_ref) = refs[:-3], refs[-3:]
    row_total, tok_count = placed_ref.shape
    expert_count, piece_rows = row_total // slot_count, out_refs[0].shape[0]

    @pl.when(pl.program_id(0) == 0)
    def _():
        expert_ids = experts_at(expert_count, tok_count, outer, own_ref[0])
        keys = slot_keys(route_ref, expert_ids)
        slots = lax.broadcasted_iota(jnp.int32, (slot_count, tok_count), 0)
        if scaled:
            gates = expert_gates(route_ref, gate_ref, expert_ids)
        for e in range(expert_count):
            here = pl.ds(e * slot_count, slot_count)
            matched = keys[e : e + 1, :] == slots
            placed_ref[here, :] = matched.astype(jnp.float32).astype(jnp.bfloat16)
            if scaled:
                gain_ref[here, :] = jnp.sum(
                    jnp.where(matched, gates[e : e + 1, :], 0.0), axis=1, keepdims=True
                )
        table_ref[...] = placed_ref[...]

    picked = jnp.dot(placed_ref[...], rows_ref[...], preferred_element_type=jnp.float32)
    if scaled:
        picked = gain_ref[...] * picked
    picked = picked.astype(jnp.bfloat16)
    for e, out_ref in enumerate(out_refs):
        out_ref[...] = picked[e * piece_rows : (e + 1) * piece_rows]


def gather_rows(own, routes, gates, rows, expert_count, slot_count, scaled, pieces, outer, held=()):
    tok_count, width = rows.shape
    row_total = expert_count * slot_count
    piece_rows = row_total // pieces
    block = tile_width(width, 1792)
    whole = pl.BlockSpec(routes.shape, lambda i: (0, 0))
    return pl.pallas_call(
        functools.partial(gather_kernel, scaled, slot_count, outer, len(held)),
        grid=(width // block,),
        in_specs=[
            pl.BlockSpec(memory_space=pltpu.SMEM),
            whole,
            whole,
            pl.BlockSpec((tok_count, block), lambda i: (0, i)),
        ]
        + [pl.BlockSpec(memory_space=pl.ANY)] * len(held),
        out_specs=[pl.BlockSpec((piece_rows, block), lambda i: (0, i))] * pieces
        + [pl.BlockSpec((row_total, tok_count), lambda i: (0, 0))],
        out_shape=[jax.ShapeDtypeStruct((piece_rows, width), jnp.bfloat16)] * pieces
        + [jax.ShapeDtypeStruct((row_total, tok_count), jnp.bfloat16)],
        scratch_shapes=[
            pltpu.VMEM((row_total, tok_count), jnp.bfloat16),
            pltpu.VMEM((row_total, 1), jnp.float32),
        ],
        compiler_params=pltpu.CompilerParams(vmem_limit_bytes=VMEM_BYTES if held else None),
        cost_estimate=pl.CostEstimate(
            flops=2 * row_total * tok_count * width,
            bytes_accessed=2 * (tok_count + row_total) * width,
            transcendentals=0,
        ),
    )(own, routes, gates, rows, *held)


def combine_kernel(weighted, expert_count, outer, own_ref, route_ref, gate_ref, *refs):
    row_refs, (out_ref, weight_ref) = refs[:-2], refs[-2:]
    row_total, tok_count = weight_ref.shape[-2:]
    slot_count = row_total // expert_count

    @pl.when(pl.program_id(0) == 0)
    def _():
        expert_ids = experts_at(expert_count, tok_count, outer, own_ref[0])
        keys = slot_keys(route_ref, expert_ids)
        slots = lax.broadcasted_iota(jnp.int32, (slot_count, tok_count), 0)
        if weighted:
            gates = expert_gates(route_ref, gate_ref, expert_ids)
        for e in range(expert_count):
            here = pl.ds(e * slot_count, slot_count)
            matched = keys[e : e + 1, :] == slots
            if not weighted:
                weight_ref[0, here, :] = matched.astype(jnp.float32).astype(jnp.bfloat16)
                continue
            left = jnp.where(matched, gates[e : e + 1, :], 0.0)
            for part in range(weight_ref.shape[0]):
                term = left.astype(jnp.bfloat16)
                weight_ref[part, here, :] = term
                left = left - term.astype(jnp.float32)

    rows = jnp.concatenate([ref[...] for ref in row_refs]) if row_refs[1:] else row_refs[0][...]
    total = None
    for part in range(weight_ref.shape[0]):
        term = lax.dot_general(
            weight_ref[part], rows, (((0,), (0,)), ((), ())), preferred_element_type=jnp.float32
        )
        total = term if total is None else total + term
    out_ref[...] = total.astype(jnp.bfloat16)


def combine_rows(own, routes, gates, pieces, expert_count, weighted, outer):
    tok_count = routes.shape[1]
    row_total, width = sum(piece.shape[0] for piece in pieces), pieces[0].shape[1]
    block = tile_width(width, 1792)
    whole = pl.BlockSpec(routes.shape, lambda i: (0, 0))
    parts = 3 if weighted else 1
    return pl.pallas_call(
        functools.partial(combine_kernel, weighted, expert_count, outer),
        grid=(width // block,),
        in_specs=[pl.BlockSpec(memory_space=pltpu.SMEM), whole, whole]
        + [pl.BlockSpec((piece.shape[0], block), lambda i: (0, i)) for piece in pieces],
        out_specs=pl.BlockSpec((tok_count, block), lambda i: (0, i)),
        out_shape=jax.ShapeDtypeStruct((tok_count, width), jnp.bfloat16),
        scratch_shapes=[pltpu.VMEM((parts, row_total, tok_count), jnp.bfloat16)],
        compiler_params=pltpu.CompilerParams(vmem_limit_bytes=VMEM_BYTES),
        cost_estimate=pl.CostEstimate(
            flops=2 * parts * row_total * tok_count * width,
            bytes_accessed=2 * (tok_count + row_total) * width,
            transcendentals=0,
        ),
    )(own, routes, gates, *pieces)


def activate(hidden, half_width):
    gate_part = hidden[:, :half_width]
    up_part = hidden[:, half_width:]
    return (gate_part * jax.nn.sigmoid(gate_part) * up_part).astype(jnp.bfloat16)


def activate_grad(hidden, act_grad, half_width):
    gate_part = hidden[:, :half_width]
    up_part = hidden[:, half_width:]
    sigmoid_gate = jax.nn.sigmoid(gate_part)
    gate_grad = act_grad * up_part * sigmoid_gate * (1.0 + gate_part * (1.0 - sigmoid_gate))
    up_grad = act_grad * gate_part * sigmoid_gate
    return jnp.concatenate([gate_grad, up_grad], axis=1).astype(jnp.bfloat16)


def hold_kernel(count, *refs):
    copies = [
        pltpu.make_async_copy(refs[k], refs[count + k], refs[2 * count].at[k]) for k in range(count)
    ]
    for copy in copies:
        copy.start()
    for copy in copies:
        copy.wait()


def hold(*arrays):
    count = len(arrays)
    return pl.pallas_call(
        functools.partial(hold_kernel, count),
        in_specs=[pl.BlockSpec(memory_space=pl.ANY)] * count,
        out_specs=[pl.BlockSpec(memory_space=pltpu.VMEM)] * count,
        out_shape=[pltpu.VMEM(a.shape, a.dtype) for a in arrays],
        scratch_shapes=[pltpu.SemaphoreType.DMA((count,))],
        compiler_params=pltpu.CompilerParams(vmem_limit_bytes=VMEM_BYTES),
        cost_estimate=pl.CostEstimate(
            flops=0, bytes_accessed=4 * sum(a.size for a in arrays), transcendentals=0
        ),
    )(*arrays)


def column_kernel(first, left_ref, right_ref, out_ref):
    width = out_ref.shape[1]
    out_ref[...] = jnp.dot(
        left_ref[...], right_ref[:, first : first + width], preferred_element_type=jnp.float32
    ).astype(jnp.bfloat16)


def part_product(kernel, left, right, first, width):
    row_total, depth = left.shape
    return pl.pallas_call(
        functools.partial(kernel, first),
        in_specs=[pl.BlockSpec(memory_space=pltpu.VMEM)] * 2,
        out_specs=pl.BlockSpec(memory_space=pltpu.VMEM),
        out_shape=jax.ShapeDtypeStruct((row_total, width), jnp.bfloat16),
        compiler_params=pltpu.CompilerParams(vmem_limit_bytes=VMEM_BYTES),
        cost_estimate=pl.CostEstimate(
            flops=2 * row_total * depth * width,
            bytes_accessed=2 * (row_total + width) * depth + 2 * row_total * width,
            transcendentals=0,
        ),
    )(left, right)


def sum_kernel(placed_ref, *refs):
    out_ref = refs[-1]
    rows = jnp.concatenate([ref[...] for ref in refs[:-1]])
    out_ref[...] = lax.dot_general(
        placed_ref[...], rows, (((0,), (0,)), ((), ())), preferred_element_type=jnp.float32
    ).astype(jnp.bfloat16)


def sum_rows(placed, pieces):
    row_total, tok_count = placed.shape
    width = pieces[0].shape[1]
    block = tile_width(width, 1792)
    return pl.pallas_call(
        sum_kernel,
        grid=(width // block,),
        in_specs=[pl.BlockSpec(placed.shape, lambda i: (0, 0))]
        + [pl.BlockSpec((piece.shape[0], block), lambda i: (0, i)) for piece in pieces],
        out_specs=pl.BlockSpec((tok_count, block), lambda i: (0, i)),
        out_shape=jax.ShapeDtypeStruct((tok_count, width), jnp.bfloat16),
        compiler_params=pltpu.CompilerParams(vmem_limit_bytes=VMEM_BYTES),
        cost_estimate=pl.CostEstimate(
            flops=2 * row_total * tok_count * width,
            bytes_accessed=2 * (tok_count + row_total) * width,
            transcendentals=0,
        ),
    )(placed, *pieces)


def held_kernel(right_dim, block, groups, left_ref, right_ref, *out_refs):
    here = pl.ds(pl.multiple_of(pl.program_id(0) * block, block), block)
    right = right_ref[here, :] if right_dim == 1 else right_ref[:, here]
    rows = lax.dot_general(
        left_ref[...], right, (((1,), (right_dim,)), ((), ())), preferred_element_type=jnp.float32
    ).astype(jnp.bfloat16)
    run = rows.shape[0] // (len(out_refs) * groups)
    for p, out_ref in enumerate(out_refs):
        for g in range(groups):
            first = (g * len(out_refs) + p) * run
            out_ref[g * run : (g + 1) * run, :] = rows[first : first + run]


def held_product(left, right, right_dim, limit, pieces, groups):
    row_total, depth = left.shape
    width = right.shape[1 - right_dim]
    block = tile_width(width, limit)
    piece_rows = row_total // pieces
    return pl.pallas_call(
        functools.partial(held_kernel, right_dim, block, groups),
        grid=(width // block,),
        in_specs=[
            pl.BlockSpec((row_total, depth), lambda i: (0, 0)),
            pl.BlockSpec(memory_space=pltpu.VMEM),
        ],
        out_specs=[pl.BlockSpec((piece_rows, block), lambda i: (0, i))] * pieces,
        out_shape=[jax.ShapeDtypeStruct((piece_rows, width), jnp.bfloat16)] * pieces,
        compiler_params=pltpu.CompilerParams(vmem_limit_bytes=VMEM_BYTES),
        cost_estimate=pl.CostEstimate(
            flops=2 * row_total * depth * width,
            bytes_accessed=2 * (row_total + width) * depth + 2 * row_total * width,
            transcendentals=0,
        ),
    )(left, right)


def cot_kernel(first, left_ref, right_ref, out_ref):
    width = out_ref.shape[1]
    out_ref[...] = lax.dot_general(
        left_ref[...],
        right_ref[first : first + width, :],
        (((1,), (1,)), ((), ())),
        preferred_element_type=jnp.float32,
    ).astype(jnp.bfloat16)


def trade(pieces, step):
    count = lax.axis_size("expert")
    got = list(pieces)
    for k in range(len(pieces) - 1, 0, -1):
        pairs = [(i, i ^ (k * step)) for i in range(count)]
        got[k] = lax.ppermute(pieces[k], "expert", pairs)
    return got


def regroup(pieces, parts):
    rows = pieces[0].shape[0] // parts
    return [jnp.concatenate([p[k * rows : (k + 1) * rows] for p in pieces]) for k in range(parts)]


def cut(rows, parts):
    size = rows.shape[0] // parts
    return [rows[k * size : (k + 1) * size] for k in range(parts)]


def send_back(out_pieces, inner):
    moved = trade(out_pieces, inner)
    runs = [trade(regroup(run, inner), 1) for run in (moved[:1], moved[1:])]
    return [run[k] for k in range(inner) for run in runs]


def dp_swap(part):
    return lax.ppermute(part, "dp", [(0, 1), (1, 0)])


def dp_sum(part):
    return lax.psum_scatter(part, "dp", scatter_dimension=0, tiled=True).astype(jnp.float32)


def pair_sum(pairs):
    sums = [own.astype(jnp.float32) + other.astype(jnp.float32) for own, other in pairs]
    return sums[0] if len(sums) == 1 else jnp.concatenate(sums, axis=1)


def dp_spread(rows):
    if lax.axis_size("dp") == 2:
        return rows
    return lax.all_gather(rows, "dp", axis=0, tiled=True)


def middle_ring(expert_rows, scaled_cot, inner_weight, outer_weight, outer, inner):
    contract_cols = (((1,), (1,)), ((), ()))
    half_width = outer_weight.shape[0]
    part = jnp.dot(jnp.concatenate(expert_rows), inner_weight, preferred_element_type=jnp.float32)
    hidden = dp_sum(part.astype(jnp.bfloat16))
    active = dp_spread(activate(hidden, half_width))
    expert_out = jnp.dot(active, outer_weight, preferred_element_type=jnp.float32)
    out_pieces = cut(expert_out.astype(jnp.bfloat16), outer)
    back_out = send_back(out_pieces, inner)
    part = lax.dot_general(
        scaled_cot, outer_weight, contract_cols, preferred_element_type=jnp.float32
    )
    act_grad = dp_sum(part.astype(jnp.bfloat16))
    hidden_cot = dp_spread(activate_grad(hidden, act_grad, half_width))
    row_grad = lax.dot_general(
        hidden_cot, inner_weight, contract_cols, preferred_element_type=jnp.float32
    )
    grad_pieces = regroup(cut(row_grad.astype(jnp.bfloat16), outer), inner)
    return active, hidden_cot, back_out, grad_pieces


def middle_pair(expert_rows, scaled_cot, inner_weight, outer_weight, outer, inner):
    half_width = outer_weight.shape[0]
    inner_weight, outer_weight = hold(inner_weight, outer_weight)
    sides, actives, out_pieces = [], [], []
    for at, rows in enumerate(expert_rows):
        sides.append([])
        for side in range(2):
            part = part_product(column_kernel, rows, inner_weight, side * half_width, half_width)
            sides[at].append((part, dp_swap(part)))
    for at, side in enumerate(sides):
        actives.append(activate(pair_sum(side), half_width))
        out_pieces += held_product(actives[at], outer_weight, 0, 512, outer // 2, 1)
    active = jnp.concatenate(actives)
    own_piece, late_sides = lax.optimization_barrier((out_pieces[0], sides))
    back_out = send_back([own_piece, *out_pieces[1:]], inner)

    chunk = half_width // CHUNKS
    pairs = []
    for at in range(CHUNKS):
        part = part_product(cot_kernel, scaled_cot, outer_weight, at * chunk, chunk)
        pairs.append((part, dp_swap(part)))
    hidden = jnp.concatenate([pair_sum(side) for side in late_sides])
    hidden_cot = activate_grad(hidden, pair_sum(pairs), half_width)
    grad_pieces = held_product(hidden_cot, inner_weight, 1, 512, inner, outer)
    return active, hidden_cot, back_out, grad_pieces


def body(tokens, cotangent, routing, gate_values, hidden_weight, output_weight):
    tok_count, _ = tokens.shape
    pick_count = routing.shape[1]
    expert_count = lax.axis_size("expert")
    slot_count = 2 * tok_count * pick_count // ROUTED
    contract_rows = (((0,), (0,)), ((), ()))
    outer = 1 << ((expert_count.bit_length() - 1) // 2)
    inner = expert_count // outer
    own = lax.axis_index("expert").astype(jnp.int32)
    routes, gates = routing.T, gate_values.T
    inner_weight = hidden_weight[0]
    outer_weight = output_weight[0]
    table = (routes, gates)

    mine = own[None]
    *token_pieces, placed = gather_rows(
        mine, *table, tokens, expert_count, slot_count, False, outer, 1
    )
    moved = trade(token_pieces, inner)
    expert_rows = []
    for run in (moved[: outer // 2], moved[outer // 2 :]):
        run = regroup(run, inner)
        run = trade(run, 1)
        expert_rows.append(jnp.concatenate(regroup(run, outer // 2)))

    cot = gather_rows(mine, *table, cotangent, expert_count, slot_count, True, inner, outer)[:-1]
    cot = trade(cot, 1)
    cot = regroup(cot, outer)
    scaled_cot = jnp.concatenate(trade(cot, inner))

    middle = middle_pair if lax.axis_size("dp") == 2 else middle_ring
    active, hidden_cot, back_out, grad_pieces = middle(
        expert_rows, scaled_cot, inner_weight, outer_weight, outer, inner
    )
    grad_pieces = trade(grad_pieces, 1)
    runs = []
    for part in (grad_pieces[: inner // 2], grad_pieces[inner // 2 :]):
        part = regroup(part, outer)
        runs.append(trade(part, inner))
    back_grad = [run[k] for k in range(outer) for run in runs]

    output_grad = lax.dot_general(
        active, scaled_cot, contract_rows, preferred_element_type=jnp.float32
    ).astype(jnp.bfloat16)
    hidden_grad = lax.dot_general(
        jnp.concatenate(expert_rows), hidden_cot, contract_rows, preferred_element_type=jnp.float32
    ).astype(jnp.bfloat16)
    mixed = combine_rows(mine, *table, back_out, expert_count, True, outer)
    token_grad = sum_rows(placed, back_grad)
    return (mixed, token_grad, hidden_grad[None], output_grad[None])


CHUNKS = 2


def solution(mesh):
    return jax.shard_map(
        body,
        mesh=mesh,
        in_specs=(
            P("expert", "dp"),
            P("expert", "dp"),
            P("expert", None),
            P("expert", None),
            P("expert", "dp", None),
            P("expert", None, "dp"),
        ),
        out_specs=(
            P("expert", "dp"),
            P("expert", "dp"),
            P("expert", "dp", None),
            P("expert", None, "dp"),
        ),
        check_vma=False,
    )
```
